128 devices in a mesh: frame: 32 (over y, x, core), tile: 4 (over z).
Axes of the slice: x: 4, y: 4, z: 4, core: 2. Of those that a mesh axis runs over, the one named last changes fastest.
Arguments:
- counts: float32 [1024, 524288], P('frame', 'tile'), may hold values from -1 to 23
- dark_level: float32 [524288], P('tile'), may hold values from 0 to 2
- flat_field: float32 [524288], P('tile'), may hold values from 0.5 to 2
- valid_pixel: int32 [524288], P('tile'), may hold values 0 or 1
- cycle_label: int32 [524288], P('tile'), may hold values from 0 to 32, as said below
- cycle_order: int32 [4, 32, 32], P('tile'), may hold values from 0 to 1024, as said below
- age_bin: int32 [1024], replicated, may hold values from 0 to 15, never falling along the last dimension, each value on 1 to 128 neighbouring positions
Outputs:
- two_time: float32 [32, 1024, 1024], P('frame', 'tile')
- aged_correlation: float32 [32, 16, 1024], P('frame', None, 'tile')
- mean_image: float32 [4, 32, 4096], P('tile', 'frame')
The draws below stay inside these ranges and needn't reach their ends.
Inputs may be any that keep to these rules, and one draw needn't show every extreme that they name: cycle_order[t, q, :] lists distinct pixel blocks of module t (indices within the module) whose nominal cycle is q, then 131072 // 128 in the unused entries; no block is listed twice in a module; some cycle fills all entries of each module. `cycle_label`: most pixels carry the nominal cycle of the block under which cycle_order lists them.
All inputs are finite; a program needn't handle non-finite values. No bound on the sum of `valid_pixel` on one device may be relied on, other than what follows from the above.
Results may differ from the reference program's by a relative error of at most 0.0003.
Values may be sent and summed in bfloat16 or wider, within the bound.
A program may use at most 128 MiB of HBM per device.

```python
import math
import jax
import jax.numpy as jnp
import numpy as np
from jax import lax

F = 1024
BLK = 128
SLOT = 4096
NA = 16
Q = 32
MODULES = 4
PM = 131072
P_SIZE = 524288


def module_layout(key):
    keys = jax.random.split(key, 4)
    block_total = PM // BLK
    per_cycle = SLOT // BLK
    places = jax.random.permutation(keys[0], block_total).astype(jnp.int32)
    ranking = jax.random.permutation(keys[1], Q).astype(jnp.int32)
    ladder = jnp.arange(Q, dtype=jnp.int32) * (3 * per_cycle // 4) // (Q - 1) + per_cycle // 4
    sizes = ladder[ranking]
    ends = jnp.cumsum(sizes)
    begins = ends - sizes
    position = jnp.arange(block_total, dtype=jnp.int32)
    nominal_sorted = jnp.sum((position[:, None] >= ends[None, :]).astype(jnp.int32), axis=1)
    nominal_block = jnp.zeros((block_total,), jnp.int32).at[places].set(nominal_sorted)
    entry_index = jnp.arange(per_cycle, dtype=jnp.int32)[None, :]
    entry_pos = jnp.minimum(begins[:, None] + entry_index, block_total - 1)
    listing = jnp.where(entry_index < sizes[:, None], places[entry_pos], block_total)
    nominal = jnp.repeat(nominal_block, BLK)
    changed = jax.random.randint(keys[2], (PM,), 0, 8) == 0
    other = jax.random.randint(keys[3], (PM,), 0, Q + 1)
    labels = jnp.where(changed, other, nominal)
    return (listing.astype(jnp.int32), labels.astype(jnp.int32))


def geometry(key):
    module_keys = jax.random.split(jax.random.fold_in(key, 7), MODULES)
    return jax.vmap(module_layout)(module_keys)


def draw_cycle_order(key, part):
    listing, labels = geometry(key)
    return listing


def draw_cycle_label(key, part):
    listing, labels = geometry(key)
    return labels.reshape(P_SIZE)


def draw_counts(key, part):
    keys = jax.random.split(jax.random.fold_in(key, 11), 6)
    beam = jnp.where(jax.random.randint(keys[0], (F, 1), 0, 12) == 0, 0, jax.random.randint(keys[1], (F, 1), 1, 4))
    tempo = jax.random.randint(keys[2], (1, P_SIZE), 0, 4)
    hold = jnp.left_shift(jnp.full((1, P_SIZE), 4, jnp.int32), 2 * tempo)
    resets = jax.random.randint(keys[3], (F, P_SIZE), 0, hold) == 0
    frame_ids = jnp.arange(F, dtype=jnp.int32)[:, None]
    latest = lax.cummax(jnp.where(resets, frame_ids, 0), axis=0)
    table = jax.random.randint(keys[4], (F, P_SIZE), 0, 8)
    level = jnp.take_along_axis(table, latest, axis=0)
    readout = 0.5 + 0.35 * jnp.clip(jax.random.normal(keys[5], (F, P_SIZE), jnp.float32), -3.0, 3.0)
    return ((beam * level).astype(jnp.float32) + readout).astype(jnp.float32)


def set_ends(entries, own_key, low, largest):
    place = [jax.random.randint(jax.random.fold_in(own_key, axis), (), 0, length) for axis, length in enumerate(entries.shape)]
    main_axis = entries.shape.index(max(entries.shape))
    next_to = place[:main_axis] + [(place[main_axis] + 1) % entries.shape[main_axis]] + place[main_axis + 1:]
    return entries.at[tuple(place)].set(low).at[tuple(next_to)].set(largest)


def levels(rng, extent, shards, least, top_value):
    loudness, own = 1.0, jax.random.fold_in(rng, 6)
    for axis_at, blocks in shards:
        steps = jnp.exp(jax.random.uniform(jax.random.fold_in(own, axis_at), (blocks,), jnp.float32, least / len(shards), top_value / len(shards)))
        loudness = loudness * jnp.repeat(steps, extent[axis_at] // blocks).reshape([-1 if axis == axis_at else 1 for axis in range(len(extent))])
    return loudness


def profile(amount, total, reach, skew):
    loads = [(1 << 20) // math.isqrt(grade ** skew) + 1 for grade in range(2, amount + 1)]
    rest, given = total - reach - (amount - 1), [1] * (amount - 1)
    while rest > 0:
        free = [i for i in range(amount - 1) if given[i] < reach]
        mass, left = sum([loads[i] for i in free]), rest
        for i in free:
            addition = min(reach - given[i], max(1, left * loads[i] // mass), rest)
            given[i] = given[i] + addition
            rest = rest - addition
    return np.array([reach] + given)


def uneven(own_key, number_of, total, most, lean):
    if number_of == 2:
        one = jax.random.randint(own_key, (), max(1, total - most), min(most, total - 1) + 1)
        return jnp.stack([one, total - one])
    tallies = jnp.asarray(profile(number_of, total, most, lean), jnp.int32)
    pairs = (number_of - 1) // 2
    source_of, sink = tallies[1:1 + 2 * pairs:2], tallies[2:2 + 2 * pairs:2]
    margin = jnp.minimum(source_of - 1, most - sink)
    passed = jax.random.randint(jax.random.fold_in(own_key, 1), (pairs,), 0, 1 << 20) % (margin + 1)
    tallies = tallies.at[1:1 + 2 * pairs:2].set(source_of - passed).at[2:2 + 2 * pairs:2].set(sink + passed)
    return tallies[jax.random.permutation(jax.random.fold_in(own_key, 2), number_of)]


def setup_inputs(seed: int = 0) -> dict:
    arg_keys = jax.random.split(jax.random.key(seed), 8)
    return {
        "counts": draw_counts(jax.random.fold_in(arg_keys[7], 71), 0),
        "dark_level": jnp.clip(2.0 * jax.random.uniform(arg_keys[1], (P_SIZE,), jnp.float32) ** levels(arg_keys[1], (P_SIZE,), ((0, 4),), -0.2, 0.2), 0.0, 2.0),
        "flat_field": jnp.clip(jnp.exp(math.log(2.0) - 1.3862944 * jax.random.uniform(arg_keys[2], (P_SIZE,), jnp.float32) ** levels(arg_keys[2], (P_SIZE,), ((0, 4),), -0.2, 0.2)), 0.5, 2.0),
        "valid_pixel": set_ends((jax.random.randint(arg_keys[3], (P_SIZE,), 0, 16) < 15).astype(jnp.int32), jax.random.fold_in(arg_keys[3], 1), 0, 1),
        "cycle_label": draw_cycle_label(jax.random.fold_in(arg_keys[7], 71), 0),
        "cycle_order": draw_cycle_order(jax.random.fold_in(arg_keys[7], 71), 0),
        "age_bin": jnp.searchsorted(jnp.cumsum(uneven(arg_keys[6], NA, F, 2 * F // NA, 0)), jnp.arange(F), side="right").astype(jnp.int32),
    }


def band_rows(cmap_rows, row_start, age_bin):
    cycle_count, row_count, col_width = cmap_rows.shape
    padded_map = jnp.concatenate([cmap_rows, jnp.zeros_like(cmap_rows)], axis=2)
    span = col_width + row_count
    window = lax.dynamic_slice_in_dim(padded_map, row_start, span, 2)
    flattened = jnp.concatenate([window.reshape(cycle_count, row_count * span), jnp.zeros((cycle_count, row_count), jnp.float32)], axis=1)
    skewed_map = flattened.reshape(cycle_count, row_count, span + 1)[:, :, :col_width]
    age_rows = lax.dynamic_slice_in_dim(age_bin, row_start, row_count)
    onehot = (age_rows[None, :] == jnp.arange(NA, dtype=jnp.int32)[:, None]).astype(jnp.float32)
    return jnp.einsum("bi,rid->rbd", onehot, skewed_map, precision=lax.Precision.HIGHEST)


def lag_counts(age_bin, lag_start, lag_count):
    frames = age_bin.shape[0]
    lag_values = lag_start + jnp.arange(lag_count, dtype=jnp.int32)
    inside = (jnp.arange(frames, dtype=jnp.int32)[:, None] + lag_values[None, :] < frames).astype(jnp.float32)
    onehot = (age_bin[None, :] == jnp.arange(NA, dtype=jnp.int32)[:, None]).astype(jnp.float32)
    return jnp.dot(onehot, inside, precision=lax.Precision.HIGHEST)


def reference(counts, dark_level, flat_field, valid_pixel, cycle_label, cycle_order, age_bin):
    modules, cycle_total, block_count = cycle_order.shape
    slot = block_count * BLK
    frames = counts.shape[0]
    pix_module = dark_level.shape[0] // modules
    spread_order = jnp.repeat(cycle_order, BLK, axis=2)
    within = (jnp.arange(slot, dtype=jnp.int32) % BLK)[None, None, :]
    is_padding = spread_order >= pix_module // BLK
    module_base = (jnp.arange(modules, dtype=jnp.int32) * pix_module)[:, None, None]
    pixel_ids = (jnp.where(is_padding, 0, spread_order * BLK + within) + module_base).astype(jnp.int32)
    cycle_ids = jnp.arange(cycle_total, dtype=jnp.int32)[None, :, None]
    member = jnp.where(is_padding, 0.0, valid_pixel[pixel_ids].astype(jnp.float32) * (cycle_label[pixel_ids] == cycle_ids).astype(jnp.float32))
    slot_gain = flat_field[pixel_ids] * member
    slot_dark = dark_level[pixel_ids]

    def one_cycle(cycle_id):
        chosen = pixel_ids[:, cycle_id, :].reshape(-1)
        columns = jnp.take(counts, chosen, axis=1).astype(jnp.float32)
        sorted_frames = ((columns - slot_dark[:, cycle_id, :].reshape(-1)) * slot_gain[:, cycle_id, :].reshape(-1)).astype(jnp.bfloat16)
        widened = sorted_frames.astype(jnp.float32)
        gram_full = jnp.dot(sorted_frames, jnp.transpose(sorted_frames), preferred_element_type=jnp.float32)
        cycle_sums = jnp.sum(widened, axis=1)
        pixel_total = jnp.maximum(jnp.sum(member[:, cycle_id, :]), 1.0)
        clamped = jnp.maximum(cycle_sums / pixel_total, 1.0)
        cycle_map = gram_full / (pixel_total * clamped[:, None] * clamped[None, :])
        image = (jnp.sum(widened, axis=0) / frames).reshape(modules, slot)
        return cycle_map, image

    two_time, images = lax.map(one_cycle, jnp.arange(cycle_total, dtype=jnp.int32))

    def cycle_bands(cycle_map):
        return band_rows(cycle_map[None], 0, age_bin)[0]

    band_sum = lax.map(cycle_bands, two_time)
    lag_total = jnp.maximum(lag_counts(age_bin, 0, frames), 1.0)
    aged_correlation = band_sum / lag_total[None]
    mean_image = jnp.transpose(images, (1, 0, 2))
    return (two_time, aged_correlation, mean_image)
```

```python
import functools

import jax
import jax.numpy as jnp
from jax import lax
from jax.experimental import pallas as pl
from jax.experimental.pallas import tpu as pltpu
from jax.sharding import PartitionSpec as P

BLK = 128
NA = 16
QSTEP = 4
HALF = 16


def sort_kernel(order, counts, dark, flat, valid, label, out, sums, held, sem):
    c, g = pl.program_id(0), pl.program_id(1)

    def load(i):
        rows = pl.ds(i * HALF, HALF)
        return pltpu.make_async_copy(counts.at[rows, :], held.at[i], sem.at[i])

    @pl.when((c == 0) & (g == 0))
    def _():
        load(0).start()
        load(1).start()
        load(0).wait()

    @pl.when((c == 1) & (g == 0))
    def _():
        load(1).wait()

    block_total = dark.shape[0]
    blocks = order.shape[1]

    @pl.loop(0, QSTEP)
    def _(k):
        q = g * QSTEP + k
        total = jnp.zeros((1, BLK), jnp.float32)
        for b in range(blocks):
            o = order[q, b]
            at = jnp.minimum(o, block_total - 1)
            row = pl.ds(at, 1)
            listed = jnp.where(o < block_total, 1.0, 0.0).astype(jnp.float32)
            usable = jnp.where(label[row, :] == q, valid[row, :].astype(jnp.float32), 0.0) * listed
            total = total + usable
            gain = flat[row, :] * usable
            columns = held[c, :, pl.ds(pl.multiple_of(at * BLK, BLK), BLK)]
            out[k, :, b * BLK : (b + 1) * BLK] = ((columns - dark[row, :]) * gain).astype(jnp.bfloat16)
        sums[k] = total


def sort_frames(block_order, counts, dark, flat, valid, label):
    frames, pixels = counts.shape
    cycles, blocks = block_order.shape
    slot = blocks * BLK
    table = pl.BlockSpec((pixels // BLK, BLK), lambda c, g, order: (0, 0))
    return pl.pallas_call(
        sort_kernel,
        grid_spec=pltpu.PrefetchScalarGridSpec(
            num_scalar_prefetch=1,
            grid=(frames // HALF, cycles // QSTEP),
            in_specs=[pl.BlockSpec(memory_space=pl.ANY), table, table, table, table],
            out_specs=[
                pl.BlockSpec((QSTEP, HALF, slot), lambda c, g, order: (g, c, 0)),
                pl.BlockSpec((QSTEP, 1, BLK), lambda c, g, order: (g, 0, 0)),
            ],
            scratch_shapes=[
                pltpu.VMEM((frames // HALF, HALF, pixels), jnp.float32),
                pltpu.SemaphoreType.DMA((frames // HALF,)),
            ],
        ),
        out_shape=[
            jax.ShapeDtypeStruct((cycles, frames, slot), jnp.bfloat16),
            jax.ShapeDtypeStruct((cycles, 1, BLK), jnp.float32),
        ],
        compiler_params=pltpu.CompilerParams(
            dimension_semantics=("arbitrary", "arbitrary"), vmem_limit_bytes=40 << 20
        ),
        cost_estimate=pl.CostEstimate(flops=3 * frames * cycles * slot, bytes_accessed=24 << 20, transcendentals=0),
    )(block_order, counts, dark, flat, valid, label)


def finish_kernel(gram, scale_col, scale_row, bins, two_time, bands, *, axis):
    rows, width = gram.shape
    cmap = gram[...] / (scale_col[...] * scale_row[...])
    two_time[...] = cmap
    first = lax.axis_index(axis) * rows
    lane = lax.broadcasted_iota(jnp.int32, (8, width), 1)
    sub = lax.broadcasted_iota(jnp.int32, (8, width), 0)
    pieces = []
    for r in range(0, rows, 8):
        part = cmap[r : r + 8, :]
        part = jnp.where(lane >= first + r + sub, part, 0.0)
        part = pltpu.roll(part, lax.rem(width - (first + r), width), 1)
        for bit in (1, 2, 4):
            part = jnp.where((sub & bit) != 0, pltpu.roll(part, width - bit, 1), part)
        pieces.append(part)
    skewed = jnp.concatenate(pieces, axis=0)
    onehot = (bins[...] == lax.broadcasted_iota(jnp.int32, (NA, rows), 0)).astype(jnp.float32)
    bands[...] = jnp.dot(onehot, skewed, precision=lax.Precision.HIGHEST, preferred_element_type=jnp.float32)


def finish(gram, scale_col, scale_row, bins):
    rows, width = gram.shape
    return pl.pallas_call(
        functools.partial(finish_kernel, axis="tile"),
        out_shape=[
            jax.ShapeDtypeStruct((rows, width), jnp.float32),
            jax.ShapeDtypeStruct((NA, width), jnp.float32),
        ],
        in_specs=[pl.BlockSpec(memory_space=pltpu.VMEM)] * 4,
        out_specs=[pl.BlockSpec(memory_space=pltpu.VMEM)] * 2,
        compiler_params=pltpu.CompilerParams(vmem_limit_bytes=32 << 20),
    )(gram, scale_col, scale_row, bins)


def local(counts, dark_level, flat_field, valid_pixel, cycle_label, cycle_order, age_bin):
    block_total = dark_level.shape[0] // BLK
    table = (block_total, BLK)
    sorted_frames, member_sums = sort_frames(
        cycle_order[0],
        counts,
        dark_level.reshape(table),
        flat_field.reshape(table),
        valid_pixel.reshape(table),
        cycle_label.reshape(table),
    )
    exchanged = lax.all_to_all(sorted_frames, "frame", split_axis=0, concat_axis=1, tiled=True)[0]
    frames = exchanged.shape[0]
    own = lax.dynamic_slice_in_dim(member_sums, lax.axis_index("frame"), 1, 0)
    widened = exchanged.astype(jnp.float32)
    cycle_sums = jnp.sum(widened, axis=1)
    image = jnp.sum(widened, axis=0) / frames
    gram = jnp.dot(exchanged, exchanged.T, preferred_element_type=jnp.float32)
    totals, pixels = lax.psum((cycle_sums, jnp.sum(own)), "tile")
    pixel_total = jnp.maximum(pixels, 1.0)
    clamped = jnp.maximum(totals / pixel_total, 1.0)
    row_count = frames // lax.axis_size("tile")
    row_start = lax.axis_index("tile") * row_count
    gram_rows = lax.psum_scatter(gram, "tile", scatter_dimension=0, tiled=True)
    row_scale = pixel_total * lax.dynamic_slice_in_dim(clamped, row_start, row_count, 0)
    bins = lax.dynamic_slice_in_dim(age_bin, row_start, row_count, 0)
    two_time, bands = finish(gram_rows, row_scale[:, None], clamped[None, :], bins[None, :])
    band_sum = lax.psum_scatter(bands, "tile", scatter_dimension=1, tiled=True)
    lags = row_start + jnp.arange(row_count, dtype=jnp.int32)
    label = jnp.arange(NA, dtype=jnp.int32)[:, None]
    below = jnp.sum((age_bin[None, :] < label).astype(jnp.int32), axis=1)
    upto = jnp.sum((age_bin[None, :] <= label).astype(jnp.int32), axis=1)
    count = jnp.minimum(upto[:, None], frames - lags[None, :]) - below[:, None]
    lag_total = jnp.maximum(count, 1).astype(jnp.float32)
    return (two_time[None], (band_sum / lag_total)[None], image[None, None])


def solution(mesh):
    in_specs = (
        P("frame", "tile"),
        P("tile"),
        P("tile"),
        P("tile"),
        P("tile"),
        P("tile", None, None),
        P(),
    )
    out_specs = (P("frame", "tile", None), P("frame", None, "tile"), P("tile", "frame", None))
    return jax.shard_map(local, mesh=mesh, in_specs=in_specs, out_specs=out_specs, check_vma=False)
```

```python
import jax
import jax.numpy as jnp
from jax import lax
from jax.experimental import pallas as pl
from jax.experimental.pallas import tpu as pltpu
from jax.sharding import PartitionSpec as P

BLK = 128
NA = 16
QSTEP = 4
HALF = 16
MESH = pl.DeviceIdType.MESH


def sort_kernel(order, counts, dark, flat, valid, label, out, sums, held, sem):
    c, g = pl.program_id(0), pl.program_id(1)

    def load(i):
        rows = pl.ds(i * HALF, HALF)
        return pltpu.make_async_copy(counts.at[rows, :], held.at[i], sem.at[i])

    @pl.when((c == 0) & (g == 0))
    def _():
        load(0).start()
        load(1).start()
        load(0).wait()

    @pl.when((c == 1) & (g == 0))
    def _():
        load(1).wait()

    block_total = dark.shape[0]
    blocks = order.shape[1]

    @pl.loop(0, QSTEP)
    def _(k):
        q = g * QSTEP + k
        total = jnp.zeros((1, BLK), jnp.float32)
        for b in range(blocks):
            o = order[q, b]
            at = jnp.minimum(o, block_total - 1)
            row = pl.ds(at, 1)
            listed = jnp.where(o < block_total, 1.0, 0.0).astype(jnp.float32)
            usable = jnp.where(label[row, :] == q, valid[row, :].astype(jnp.float32), 0.0) * listed
            total = total + usable
            gain = flat[row, :] * usable
            columns = held[c, :, pl.ds(pl.multiple_of(at * BLK, BLK), BLK)]
            out[k, :, b * BLK : (b + 1) * BLK] = ((columns - dark[row, :]) * gain).astype(jnp.bfloat16)
        sums[k] = total


def sort_frames(block_order, counts, dark, flat, valid, label):
    frames, pixels = counts.shape
    cycles, blocks = block_order.shape
    slot = blocks * BLK
    table = pl.BlockSpec((pixels // BLK, BLK), lambda c, g, order: (0, 0))
    return pl.pallas_call(
        sort_kernel,
        grid_spec=pltpu.PrefetchScalarGridSpec(
            num_scalar_prefetch=1,
            grid=(frames // HALF, cycles // QSTEP),
            in_specs=[pl.BlockSpec(memory_space=pl.ANY), table, table, table, table],
            out_specs=[
                pl.BlockSpec((QSTEP, HALF, slot), lambda c, g, order: (g, c, 0)),
                pl.BlockSpec((QSTEP, 1, BLK), lambda c, g, order: (g, 0, 0)),
            ],
            scratch_shapes=[
                pltpu.VMEM((frames // HALF, HALF, pixels), jnp.float32),
                pltpu.SemaphoreType.DMA((frames // HALF,)),
            ],
        ),
        out_shape=[
            jax.ShapeDtypeStruct((cycles, frames, slot), jnp.bfloat16),
            jax.ShapeDtypeStruct((cycles, 1, BLK), jnp.float32),
        ],
        compiler_params=pltpu.CompilerParams(
            dimension_semantics=("arbitrary", "arbitrary"), vmem_limit_bytes=40 << 20
        ),
        cost_estimate=pl.CostEstimate(flops=3 * frames * cycles * slot, bytes_accessed=24 << 20, transcendentals=0),
    )(block_order, counts, dark, flat, valid, label)


def steps_of(k, e, h):
    dy = (0, 2)[e] if k < 2 else (1, 3)[e]
    dx = (0, 2)[h] if k % 2 == 0 else (3, 1)[h]
    return dy, dx


def contract(a, b):
    return lax.dot_general(a, b, (((1,), (1,)), ((), ())), preferred_element_type=jnp.float32)


def exchange_kernel(
    frames_in,
    members,
    ages,
    two_time,
    aged,
    image,
    x_all,
    part,
    inbox,
    total,
    shared,
    sums,
    sums_in,
    bands,
    bands_in,
    own_sem,
    xs_sem,
    xr_sem,
    ps_sem,
    pr_sem,
    hs_sem,
    hr_sem,
    ss_sem,
    sr_sem,
    bs_sem,
    br_sem,
):
    f, t = lax.axis_index("frame"), lax.axis_index("tile")
    y, x, c = f // 8, (f // 2) % 4, f % 2
    role = (y - t + 4) % 4
    odd, side = role % 2, role // 2

    def chip(dy, dx, sign):
        return (((y + sign * dy + 4) % 4) * 4 + (x + sign * dx + 4) % 4) * 2

    def tile_of(r):
        return (y - r + 4) % 4

    def frames_of(slot):
        return x_all.at[pl.ds(pl.multiple_of(slot * 32, 32), 32), :]

    def send(k, e, h, dc):
        dy, dx = steps_of(k, e, h)
        dst = chip(dy, dx, 1) + (c + dc) % 2
        m = 4 * k + 2 * e + h
        return pltpu.make_async_remote_copy(
            src_ref=frames_in.at[dst],
            dst_ref=frames_of(2 * m + c),
            send_sem=xs_sem.at[m, dc],
            recv_sem=xr_sem.at[2 * m + c],
            device_id=(dst, t),
            device_id_type=MESH,
        )

    def arrival(k, e, h, dc):
        dy, dx = steps_of(k, e, h)
        sc = (c + dc) % 2
        m = 4 * k + 2 * e + h
        return pltpu.make_async_remote_copy(
            src_ref=frames_in.at[f],
            dst_ref=frames_of(2 * m + sc),
            send_sem=xs_sem.at[m, dc],
            recv_sem=xr_sem.at[2 * m + sc],
            device_id=(chip(dy, dx, -1) + sc, t),
            device_id_type=MESH,
        )

    def quarter():
        return [(e, h, dc) for first in range(2) for dc in range(2) for e, h in ((0, first), (1, 1 - first))]

    def is_own(k, e, h, dc):
        return (k, e, h, dc) == (0, 0, 0, 0)

    barrier = pltpu.get_barrier_semaphore()
    for dy in range(4):
        for dx in range(4):
            for dc in range(2):
                if (dy, dx, dc) != (0, 0, 0):
                    peer = chip(dy, dx, 1) + (c + dc) % 2
                    pl.semaphore_signal(barrier, inc=1, device_id=(peer, t), device_id_type=MESH)
    for dz in range(1, 4):
        pl.semaphore_signal(barrier, inc=1, device_id=(f, (t + dz) % 4), device_id_type=MESH)
    pl.semaphore_wait(barrier, 34)

    own = pltpu.make_async_copy(frames_in.at[f], frames_of(c), own_sem)
    own.start()
    for k in range(2):
        for e, h, dc in quarter():
            if not is_own(k, e, h, dc):
                send(k, e, h, dc).start()

    ones = jnp.ones((8, 1024), jnp.bfloat16)
    width = x_all.shape[1]
    chunks = width // 1024
    group = lambda r, j: 4 * (r % 2) + 2 * j + r // 2

    def tile_copy(src, dst, send_sem, recv_sem, tile):
        return pltpu.make_async_remote_copy(
            src_ref=src, dst_ref=dst, send_sem=send_sem, recv_sem=recv_sem, device_id=(f, tile), device_id_type=MESH
        )

    def partial_copy(k, cg, half):
        tile = tile_of(cg // 2 + 2 * half)
        slot = 3 - (tile - t + 4) % 4
        return tile, lambda: tile_copy(
            part.at[k, cg, half],
            inbox.at[k, cg % 2, slot],
            ps_sem.at[k, cg, half],
            pr_sem.at[k, cg % 2, slot],
            tile,
        )

    def share_copy(k, j, e):
        g = group(role, j)
        return tile_copy(
            total.at[k, j, pl.ds(128 * e, 128), :],
            shared.at[k % 2, g],
            hs_sem.at[k, j, e],
            hr_sem.at[k % 2, g],
            tile_of(k // 2 + 2 * e),
        )

    def shares_to_wait(k, start):
        for j in range(2):
            for e in range(2):
                for p in range(2):
                    if 2 * p + j < k:

                        @pl.when((odd == p) & (role != k // 2 + 2 * e))
                        def _():
                            if start:
                                share_copy(k, j, e).start()
                            else:
                                share_copy(k, j, e).wait_send()

    for k in range(4):
        new = pl.ds(256 * k, 256)
        for e, h, dc in quarter():
            if is_own(k, e, h, dc):
                own.wait()
            else:
                arrival(k, e, h, dc).wait_recv()
        if k < 2:
            for e, h, dc in quarter():
                send(k + 2, e, h, dc).start()
        for cg in range(k + 1):

            def body(i, acc):
                at = pl.ds(pl.multiple_of(i * 1024, 1024), 1024)
                return acc + contract(x_all[new, at], x_all[256 * cg : 256 * cg + 256, at])

            acc = lax.fori_loop(0, chunks, body, jnp.zeros((256, 256), jnp.float32))
            for half in range(2):
                part[k, cg, half] = acc[:, 128 * half : 128 * half + 128]
            for half in range(2):
                tile, copy = partial_copy(k, cg, half)

                @pl.when(tile != t)
                def _():
                    copy().start()

        line = jnp.zeros((8, 256), jnp.float32)
        for i in range(chunks):
            line = line + contract(ones, x_all[new, i * 1024 : (i + 1) * 1024])
        sums[k, :, 0:256] = line
        sums[k, :, 256:384] = jnp.broadcast_to(members[f], (8, 128))
        for dz in range(1, 4):
            tile_copy(
                sums.at[k], sums_in.at[k, 3 - dz], ss_sem.at[k, dz - 1], sr_sem.at[k, 3 - dz], (t + dz) % 4
            ).start()
        for i in range(chunks):
            at = slice(i * 1024, (i + 1) * 1024)
            row = jnp.dot(ones[:, 0:256], x_all[new, at], preferred_element_type=jnp.float32)[0:1]
            if k == 0:
                image[:, at] = row
            elif k < 3:
                image[:, at] = image[:, at] + row
            else:
                image[:, at] = (image[:, at] + row) * (1.0 / 1024.0)

        for j in range(2):
            for p in range(2):
                cg = 2 * p + j
                if cg <= k:

                    @pl.when(odd == p)
                    def _():
                        for slot in range(3):
                            tile_copy(
                                part.at[k, cg, 0], inbox.at[k, j, slot], ps_sem.at[k, cg, 0], pr_sem.at[k, j, slot], (t + slot + 1) % 4
                            ).wait_recv()
                        total[k, j] = (part[k, cg, side] + inbox[k, j, 0]) + (inbox[k, j, 1] + inbox[k, j, 2])
                        if cg < k:
                            for e in range(2):

                                @pl.when(role == k // 2 + 2 * e)
                                def _():
                                    shared[k % 2, group(role, j)] = total[k, j, 128 * e : 128 * e + 128, :]

        shares_to_wait(k, True)

    for k in range(4):
        for slot in range(3):
            tile_copy(
                sums.at[k], sums_in.at[k, slot], ss_sem.at[k, 0], sr_sem.at[k, slot], (t + slot + 1) % 4
            ).wait_recv()
    quarters = [
        (sums[k] + sums_in[k, 0]) + (sums_in[k, 1] + sums_in[k, 2]) for k in range(4)
    ]
    pixel_total = jnp.maximum(jnp.sum(quarters[0][0:1, 256:384], axis=1, keepdims=True), 1.0)
    clamped = [jnp.maximum(qs[:, 0:256] / pixel_total, 1.0) for qs in quarters]
    lane = lax.broadcasted_iota(jnp.int32, (128, 128), 1)
    low = lane < 64

    for p in range(2):

        @pl.when(odd == p)
        def _():
            for jj in range(2):
                kk = 2 * p + jj
                mine = jnp.where(side == 0, clamped[kk][:, 0:128], clamped[kk][:, 128:256])
                row_scale = jnp.transpose(pixel_total * mine)[:, 0:1]

                def block(g):
                    kg, e = g // 2, g % 2
                    if kg < kk:

                        @pl.when(group(role, g // 2 - 2 * (g // 4)) != g)
                        def _():
                            tile_copy(
                                total.at[0, 0, pl.ds(0, 128), :], shared.at[jj, g], hs_sem.at[0, 0, 0], hr_sem.at[jj, g], (t + 1) % 4
                            ).wait_recv()

                        value = shared[jj, g]
                    else:
                        value = jnp.transpose(total[kg, jj, 128 * e : 128 * e + 128, :])
                    return value / (row_scale * clamped[kg][0:1, 128 * e : 128 * e + 128])

                for r in range(4):
                    a = block(4 * (r % 2) + r // 2)
                    b = block(4 * (r % 2) + r // 2 + 2)
                    first = jnp.where(low, a, pltpu.roll(b, 64, 1))
                    second = jnp.where(low, pltpu.roll(a, 64, 1), b)
                    natural = pltpu.roll(jnp.concatenate([first, second], axis=1), 64 * x, 1)
                    at = pl.ds(pl.multiple_of(tile_of(r) * 256, 256), 256)
                    for h in range(2):
                        rows = pl.ds(pl.multiple_of(64 * ((x + jj + 2 * h) % 4), 64), 64)
                        two_time[rows, at] = natural[64 * h : 64 * h + 64, :]

    first = t * 256
    lane8 = lax.broadcasted_iota(jnp.int32, (8, 1024), 1)
    sub8 = lax.broadcasted_iota(jnp.int32, (8, 1024), 0)
    pieces = []
    for r in range(0, 256, 8):
        piece = two_time[r : r + 8, :]
        piece = jnp.where(lane8 >= first + r + sub8, piece, 0.0)
        piece = pltpu.roll(piece, (2048 - (first + r)) % 1024, 1)
        for bit in (1, 2, 4):
            piece = jnp.where((sub8 & bit) != 0, pltpu.roll(piece, 1024 - bit, 1), piece)
        pieces.append(piece)
    skewed = jnp.concatenate(pieces, axis=0)
    bins = ages[:, pl.ds(pl.multiple_of(first, 256), 256)]
    onehot = (bins == lax.broadcasted_iota(jnp.int32, (NA, 256), 0)).astype(jnp.float32)
    band = jnp.dot(onehot, skewed, precision=lax.Precision.HIGHEST, preferred_element_type=jnp.float32)
    for r in range(4):
        bands[r] = band[:, 256 * r : 256 * r + 256]
    label = lax.broadcasted_iota(jnp.int32, (NA, 1024), 0)
    below = jnp.sum((ages[...] < label).astype(jnp.float32), axis=1, keepdims=True)
    upto = jnp.sum((ages[...] <= label).astype(jnp.float32), axis=1, keepdims=True)
    for dz in range(1, 4):
        peer = (t + dz) % 4
        tile_copy(bands.at[peer], bands_in.at[3 - dz], bs_sem.at[dz - 1], br_sem.at[3 - dz], peer).start()
    lags = (first + lax.broadcasted_iota(jnp.int32, (NA, 256), 1)).astype(jnp.float32)
    lag_total = jnp.maximum(jnp.minimum(upto, 1024.0 - lags) - below, 1.0)
    for slot in range(3):
        tile_copy(bands.at[0], bands_in.at[slot], bs_sem.at[0], br_sem.at[slot], (t + slot + 1) % 4).wait_recv()
    aged[...] = ((bands[t] + bands_in[0]) + (bands_in[1] + bands_in[2])) / lag_total

    for k in range(4):
        for e, h, dc in quarter():
            if not is_own(k, e, h, dc):
                send(k, e, h, dc).wait_send()
        for cg in range(k + 1):
            for half in range(2):
                tile, copy = partial_copy(k, cg, half)

                @pl.when(tile != t)
                def _():
                    copy().wait_send()

        for dz in range(1, 4):
            tile_copy(
                sums.at[k], sums_in.at[k, 3 - dz], ss_sem.at[k, dz - 1], sr_sem.at[k, 3 - dz], (t + dz) % 4
            ).wait_send()
        shares_to_wait(k, False)
    for dz in range(1, 4):
        peer = (t + dz) % 4
        tile_copy(bands.at[peer], bands_in.at[3 - dz], bs_sem.at[dz - 1], br_sem.at[3 - dz], peer).wait_send()


def exchange(sorted_frames, members, ages):
    slot = sorted_frames.shape[2]
    vmem = pl.BlockSpec(memory_space=pltpu.VMEM)
    f32 = jnp.float32
    dma = pltpu.SemaphoreType.DMA
    return pl.pallas_call(
        exchange_kernel,
        out_shape=[
            jax.ShapeDtypeStruct((256, 1024), f32),
            jax.ShapeDtypeStruct((NA, 256), f32),
            jax.ShapeDtypeStruct((1, slot), f32),
        ],
        in_specs=[pl.BlockSpec(memory_space=pl.ANY), vmem, vmem],
        out_specs=[vmem] * 3,
        scratch_shapes=[
            pltpu.VMEM((1024, slot), jnp.bfloat16),
            pltpu.VMEM((4, 4, 2, 256, 128), f32),
            pltpu.VMEM((4, 2, 3, 256, 128), f32),
            pltpu.VMEM((4, 2, 256, 128), f32),
            pltpu.VMEM((2, 8, 128, 128), f32),
            pltpu.VMEM((4, 8, 384), f32),
            pltpu.VMEM((4, 3, 8, 384), f32),
            pltpu.VMEM((4, NA, 256), f32),
            pltpu.VMEM((3, NA, 256), f32),
            dma(()),
            dma((16, 2)),
            dma((32,)),
            dma((4, 4, 2)),
            dma((4, 2, 3)),
            dma((4, 2, 2)),
            dma((2, 8)),
            dma((4, 3)),
            dma((4, 3)),
            dma((3,)),
            dma((3,)),
        ],
        compiler_params=pltpu.CompilerParams(collective_id=0, has_side_effects=True, vmem_limit_bytes=44 << 20),
    )(sorted_frames, members, ages)


def local(counts, dark_level, flat_field, valid_pixel, cycle_label, cycle_order, age_bin):
    block_total = dark_level.shape[0] // BLK
    table = (block_total, BLK)
    sorted_frames, member_sums = sort_frames(
        cycle_order[0],
        counts,
        dark_level.reshape(table),
        flat_field.reshape(table),
        valid_pixel.reshape(table),
        cycle_label.reshape(table),
    )
    two_time, aged, image = exchange(sorted_frames, member_sums, age_bin[None, :])
    return (two_time[None], aged[None], image[None])


def solution(mesh):
    in_specs = (
        P("frame", "tile"),
        P("tile"),
        P("tile"),
        P("tile"),
        P("tile"),
        P("tile", None, None),
        P(),
    )
    out_specs = (P("frame", "tile", None), P("frame", None, "tile"), P("tile", "frame", None))
    return jax.shard_map(local, mesh=mesh, in_specs=in_specs, out_specs=out_specs, check_vma=False)
```

```python
import jax
import jax.numpy as jnp
from jax import lax
from jax.experimental import pallas as pl
from jax.experimental.pallas import tpu as pltpu
from jax.sharding import PartitionSpec as P

BLK = 128
NA = 16
AHEAD = 5
QSTEP = 4
ROWS = 32
MESH = pl.DeviceIdType.MESH


def sort_kernel(order, counts, dark, flat, valid, label, out, sums, held, sem):
    g = pl.program_id(0)

    @pl.when(g == 0)
    def _():
        loads = []
        for r in range(4):
            rows = pl.ds(8 * r, 8)
            loads.append(pltpu.make_async_copy(counts.at[rows, :], held.at[rows, :], sem.at[r]))
        for load in loads:
            load.start()
        for load in loads:
            load.wait()

    block_total = dark.shape[0]
    blocks = order.shape[1]

    @pl.loop(0, QSTEP)
    def _(k):
        q = g * QSTEP + k
        total = jnp.zeros((1, BLK), jnp.float32)
        for b in range(blocks):
            o = order[q, b]
            at = jnp.minimum(o, block_total - 1)
            row = pl.ds(at, 1)
            listed = jnp.where(o < block_total, 1.0, 0.0).astype(jnp.float32)
            usable = jnp.where(label[row, :] == q, valid[row, :].astype(jnp.float32), 0.0) * listed
            total = total + usable
            gain = flat[row, :] * usable
            columns = held[:, pl.ds(pl.multiple_of(at * BLK, BLK), BLK)]
            out[k, :, b * BLK : (b + 1) * BLK] = ((columns - dark[row, :]) * gain).astype(jnp.bfloat16)
        sums[k] = total


def sort_frames(block_order, counts, dark, flat, valid, label):
    frames, pixels = counts.shape
    cycles, blocks = block_order.shape
    slot = blocks * BLK
    table = pl.BlockSpec((pixels // BLK, BLK), lambda g, order: (0, 0))
    return pl.pallas_call(
        sort_kernel,
        grid_spec=pltpu.PrefetchScalarGridSpec(
            num_scalar_prefetch=1,
            grid=(cycles // QSTEP,),
            in_specs=[pl.BlockSpec(memory_space=pl.ANY), table, table, table, table],
            out_specs=[
                pl.BlockSpec((QSTEP, frames, slot), lambda g, order: (g, 0, 0)),
                pl.BlockSpec((QSTEP, 1, BLK), lambda g, order: (g, 0, 0)),
            ],
            scratch_shapes=[
                pltpu.VMEM((frames, pixels), jnp.float32),
                pltpu.SemaphoreType.DMA((4,)),
            ],
        ),
        out_shape=[
            jax.ShapeDtypeStruct((cycles, frames, slot), jnp.bfloat16),
            jax.ShapeDtypeStruct((cycles, 1, BLK), jnp.float32),
        ],
        compiler_params=pltpu.CompilerParams(
            dimension_semantics=("arbitrary",), vmem_limit_bytes=60 << 20
        ),
        cost_estimate=pl.CostEstimate(flops=3 * frames * cycles * slot, bytes_accessed=24 << 20, transcendentals=0),
    )(block_order, counts, dark, flat, valid, label)


def steps_of(k, e, h):
    dy = (0, 2)[e] if k < 2 else (1, 3)[e]
    dx = (0, 2)[h] if k % 2 == 0 else (3, 1)[h]
    return dy, dx


def contract(a, b):
    return lax.dot_general(a, b, (((1,), (1,)), ((), ())), preferred_element_type=jnp.float32)


def exchange_kernel(
    frames_in,
    members,
    ages,
    two_time,
    aged,
    image,
    x_all,
    part,
    inbox,
    total,
    shared,
    sums,
    sums_in,
    bands,
    bands_in,
    own_sem,
    xs_sem,
    xr_sem,
    ps_sem,
    pr_sem,
    hs_sem,
    hr_sem,
    ss_sem,
    sr_sem,
    bs_sem,
    br_sem,
):
    f, t = lax.axis_index("frame"), lax.axis_index("tile")
    y, x, c = f // 8, (f // 2) % 4, f % 2
    role = (y - t + 4) % 4
    odd, side = role % 2, role // 2

    def chip(dy, dx, sign):
        return (((y + sign * dy + 4) % 4) * 4 + (x + sign * dx + 4) % 4) * 2

    def tile_of(r):
        return (y - r + 4) % 4

    def frames_of(slot):
        return x_all.at[pl.ds(pl.multiple_of(slot * 32, 32), 32), :]

    def send(k, e, h, dc):
        dy, dx = steps_of(k, e, h)
        dst = chip(dy, dx, 1) + (c + dc) % 2
        m = 4 * k + 2 * e + h
        return pltpu.make_async_remote_copy(
            src_ref=frames_in.at[dst],
            dst_ref=frames_of(2 * m + c),
            send_sem=xs_sem.at[m, dc],
            recv_sem=xr_sem.at[2 * m + c],
            device_id=(dst, t),
            device_id_type=MESH,
        )

    def arrival(k, e, h, dc):
        dy, dx = steps_of(k, e, h)
        sc = (c + dc) % 2
        m = 4 * k + 2 * e + h
        return pltpu.make_async_remote_copy(
            src_ref=frames_in.at[f],
            dst_ref=frames_of(2 * m + sc),
            send_sem=xs_sem.at[m, dc],
            recv_sem=xr_sem.at[2 * m + sc],
            device_id=(chip(dy, dx, -1) + sc, t),
            device_id_type=MESH,
        )

    def pair(p):
        k, first = p // 2, p % 2
        chips = {4: ((1, 0), (0, 1)), 5: ((0, 0), (1, 1))}.get(p, ((0, first), (1, 1 - first)))
        return [(k, e, h, dc) for dc in range(2) for e, h in chips if (k, e, h, dc) != (0, 0, 0, 0)]

    def send_pair(p):
        for who in pair(p):
            send(*who).start()

    barrier = pltpu.get_barrier_semaphore()
    for dy in range(4):
        for dx in range(4):
            for dc in range(2):
                if (dy, dx, dc) != (0, 0, 0):
                    peer = chip(dy, dx, 1) + (c + dc) % 2
                    pl.semaphore_signal(barrier, inc=1, device_id=(peer, t), device_id_type=MESH)
    for dz in range(1, 4):
        pl.semaphore_signal(barrier, inc=1, device_id=(f, (t + dz) % 4), device_id_type=MESH)
    pl.semaphore_wait(barrier, 34)

    own = pltpu.make_async_copy(frames_in.at[f], frames_of(c), own_sem)
    own.start()
    for p in range(AHEAD):
        send_pair(p)

    ones = jnp.ones((8, 1024), jnp.bfloat16)
    chunks = x_all.shape[1] // 1024
    group = lambda r, j: 4 * (r % 2) + 2 * j + r // 2

    def tile_copy(src, dst, send_sem, recv_sem, tile):
        return pltpu.make_async_remote_copy(
            src_ref=src, dst_ref=dst, send_sem=send_sem, recv_sem=recv_sem, device_id=(f, tile), device_id_type=MESH
        )

    def pieces_of(k, cg):
        if k < 3 or cg == 3:
            return [(0, 256, 2 * k + 1)]
        return [(0, 64, 6), (192, 64, 6), (64, 128, 7)]

    def part_send(k, cg, half, i):
        tile = tile_of(cg // 2 + 2 * half)
        slot = 3 - (tile - t + 4) % 4
        at, n, _ = pieces_of(k, cg)[i]
        return tile, lambda: tile_copy(
            part.at[k, cg, half, pl.ds(at, n), :],
            inbox.at[k, cg % 2, slot, pl.ds(at, n), :],
            ps_sem.at[k, cg, half, i],
            pr_sem.at[k, cg % 2, slot, i],
            tile,
        )

    def start_parts(k, cg, phase):
        for half in range(2):
            for i, piece in enumerate(pieces_of(k, cg)):
                if piece[2] == phase:
                    tile, copy = part_send(k, cg, half, i)

                    @pl.when(tile != t)
                    def _():
                        copy().start()

    def strip(k, cg, phase):
        rows = [pl.ds(256 * k + at, n) for at, n, when in pieces_of(k, cg) if when == phase]
        height = sum(n for at, n, when in pieces_of(k, cg) if when == phase)

        def body(i, acc):
            at = pl.ds(pl.multiple_of(i * 1024, 1024), 1024)
            new = [x_all[r, at] for r in rows]
            new = new[0] if len(new) == 1 else jnp.concatenate(new, axis=0)
            return acc + contract(new, x_all[256 * cg : 256 * cg + 256, at])

        acc = lax.fori_loop(0, chunks, body, jnp.zeros((height, 256), jnp.float32))
        done = 0
        for at, n, when in pieces_of(k, cg):
            if when == phase:
                for half in range(2):
                    part[k, cg, half, at : at + n, :] = acc[done : done + n, 128 * half : 128 * half + 128]
                done += n
        start_parts(k, cg, phase)

    def segments(k, phase):
        if k < 3:
            return [(0, 128), (128, 128)] if phase == 2 * k + 1 else []
        return [(0, 64), (192, 64)] if phase == 6 else [(64, 64), (128, 64)]

    def share_copy(k, j, at, n):
        g = group(role, j)
        i = at // 64
        return tile_copy(
            total.at[k, j, pl.ds(at, n), :],
            shared.at[k % 2, g, pl.ds(at % 128, n), :],
            hs_sem.at[k, j, i],
            hr_sem.at[k % 2, g, i % 2],
            tile_of(k // 2 + 2 * (at // 128)),
        )

    def reduce_parts(k, phase):
        for j in range(2):
            for p in range(2):
                cg = 2 * p + j
                pieces = [(i, at, n) for i, (at, n, when) in enumerate(pieces_of(k, cg)) if when == phase]
                if cg <= k and pieces:

                    @pl.when(odd == p)
                    def _():
                        for i, at, n in pieces:
                            rows = pl.ds(at, n)
                            for slot in range(3):
                                tile_copy(
                                    part.at[k, cg, 0, rows, :],
                                    inbox.at[k, j, slot, rows, :],
                                    ps_sem.at[k, cg, 0, i],
                                    pr_sem.at[k, j, slot, i],
                                    (t + slot + 1) % 4,
                                ).wait_recv()
                            total[k, j, rows, :] = (part[k, cg, side, rows, :] + inbox[k, j, 0, rows, :]) + (
                                inbox[k, j, 1, rows, :] + inbox[k, j, 2, rows, :]
                            )

        shares(k, phase, True)

    def shares(k, phase, start):
        for j in range(2):
            for p in range(2):
                if 2 * p + j < k:
                    for at, n in segments(k, phase):
                        owner = k // 2 + 2 * (at // 128)

                        @pl.when((odd == p) & (role != owner))
                        def _():
                            if start:
                                share_copy(k, j, at, n).start()
                            else:
                                share_copy(k, j, at, n).wait_send()

                        if start:

                            @pl.when((odd == p) & (role == owner))
                            def _():
                                shared[k % 2, group(role, j), at % 128 : at % 128 + n, :] = total[k, j, at : at + n, :]

    def sums_copy(k, dz):
        return tile_copy(sums.at[k], sums_in.at[k, 3 - dz], ss_sem.at[k, dz - 1], sr_sem.at[k, 3 - dz], (t + dz) % 4)

    def frame_sums(k):
        new = pl.ds(256 * k, 256)
        line = jnp.zeros((8, 256), jnp.float32)
        for i in range(chunks):
            line = line + contract(ones, x_all[new, i * 1024 : (i + 1) * 1024])
        sums[k, :, 0:256] = line
        sums[k, :, 256:384] = jnp.broadcast_to(members[f], (8, 128))
        for i in range(chunks):
            at = slice(i * 1024, (i + 1) * 1024)
            row = jnp.dot(ones[:, 0:256], x_all[new, at], preferred_element_type=jnp.float32)[0:1]
            if k == 0:
                image[:, at] = row
            elif k < 3:
                image[:, at] = image[:, at] + row
            else:
                image[:, at] = (image[:, at] + row) * (1.0 / 1024.0)
        for dz in range(1, 4):
            sums_copy(k, dz).start()

    for p in range(8):
        k = p // 2
        for who in pair(p):
            arrival(*who).wait_recv()
        if p == 0:
            own.wait()
        if p + AHEAD < 8:
            send_pair(p + AHEAD)
        for cg in range(k + 1):
            if any(when == p for at, n, when in pieces_of(k, cg)):
                strip(k, cg, p)
        if p % 2 == 0 and p > 0:
            frame_sums(k - 1)
            reduce_parts(k - 1, p - 1)
        if p == 6:
            reduce_parts(3, 6)
    frame_sums(3)
    reduce_parts(3, 7)

    for k in range(4):
        for slot in range(3):
            tile_copy(
                sums.at[k], sums_in.at[k, slot], ss_sem.at[k, 0], sr_sem.at[k, slot], (t + slot + 1) % 4
            ).wait_recv()
    quarters = [
        (sums[k] + sums_in[k, 0]) + (sums_in[k, 1] + sums_in[k, 2]) for k in range(4)
    ]
    pixel_total = jnp.maximum(jnp.sum(quarters[0][0:1, 256:384], axis=1, keepdims=True), 1.0)
    clamped = [jnp.maximum(qs[:, 0:256] / pixel_total, 1.0) for qs in quarters]
    lane = lax.broadcasted_iota(jnp.int32, (128, 128), 1)
    low = lane < 64

    for p in range(2):

        @pl.when(odd == p)
        def _():
            for jj in range(2):
                kk = 2 * p + jj
                mine = jnp.where(side == 0, clamped[kk][:, 0:128], clamped[kk][:, 128:256])
                row_scale = jnp.transpose(pixel_total * mine)[:, 0:1]

                def block(g):
                    kg, e = g // 2, g % 2
                    if kg < kk:

                        @pl.when(group(role, g // 2 - 2 * (g // 4)) != g)
                        def _():
                            n = 64 if kk == 3 else 128
                            for i in range(128 // n):
                                rows = pl.ds(i * n, n)
                                tile_copy(
                                    total.at[0, 0, rows, :],
                                    shared.at[jj, g, rows, :],
                                    hs_sem.at[0, 0, 0],
                                    hr_sem.at[jj, g, i],
                                    (t + 1) % 4,
                                ).wait_recv()

                        value = shared[jj, g]
                    else:
                        value = jnp.transpose(total[kg, jj, 128 * e : 128 * e + 128, :])
                    return value / (row_scale * clamped[kg][0:1, 128 * e : 128 * e + 128])

                for r in range(4):
                    a = block(4 * (r % 2) + r // 2)
                    b = block(4 * (r % 2) + r // 2 + 2)
                    first = jnp.where(low, a, pltpu.roll(b, 64, 1))
                    second = jnp.where(low, pltpu.roll(a, 64, 1), b)
                    natural = pltpu.roll(jnp.concatenate([first, second], axis=1), 64 * x, 1)
                    at = pl.ds(pl.multiple_of(tile_of(r) * 256, 256), 256)
                    for h in range(2):
                        rows = pl.ds(pl.multiple_of(64 * ((x + jj + 2 * h) % 4), 64), 64)
                        two_time[rows, at] = natural[64 * h : 64 * h + 64, :]

    first = t * 256
    lane8 = lax.broadcasted_iota(jnp.int32, (8, 1024), 1)
    sub8 = lax.broadcasted_iota(jnp.int32, (8, 1024), 0)
    pieces = []
    for r in range(0, 256, 8):
        piece = two_time[r : r + 8, :]
        piece = jnp.where(lane8 >= first + r + sub8, piece, 0.0)
        piece = pltpu.roll(piece, (2048 - (first + r)) % 1024, 1)
        for bit in (1, 2, 4):
            piece = jnp.where((sub8 & bit) != 0, pltpu.roll(piece, 1024 - bit, 1), piece)
        pieces.append(piece)
    skewed = jnp.concatenate(pieces, axis=0)
    bins = ages[:, pl.ds(pl.multiple_of(first, 256), 256)]
    onehot = (bins == lax.broadcasted_iota(jnp.int32, (NA, 256), 0)).astype(jnp.float32)
    band = jnp.dot(onehot, skewed, precision=lax.Precision.HIGHEST, preferred_element_type=jnp.float32)
    for r in range(4):
        bands[r] = band[:, 256 * r : 256 * r + 256]
    label = lax.broadcasted_iota(jnp.int32, (NA, 1024), 0)
    below = jnp.sum((ages[...] < label).astype(jnp.float32), axis=1, keepdims=True)
    upto = jnp.sum((ages[...] <= label).astype(jnp.float32), axis=1, keepdims=True)
    for dz in range(1, 4):
        peer = (t + dz) % 4
        tile_copy(bands.at[peer], bands_in.at[3 - dz], bs_sem.at[dz - 1], br_sem.at[3 - dz], peer).start()
    lags = (first + lax.broadcasted_iota(jnp.int32, (NA, 256), 1)).astype(jnp.float32)
    lag_total = jnp.maximum(jnp.minimum(upto, 1024.0 - lags) - below, 1.0)
    for slot in range(3):
        tile_copy(bands.at[0], bands_in.at[slot], bs_sem.at[0], br_sem.at[slot], (t + slot + 1) % 4).wait_recv()
    aged[...] = ((bands[t] + bands_in[0]) + (bands_in[1] + bands_in[2])) / lag_total

    for p in range(8):
        for who in pair(p):
            send(*who).wait_send()
        for k in range(4):
            shares(k, p, False) if p == 2 * k + 1 or (k, p) == (3, 6) else None
    for k in range(4):
        for cg in range(k + 1):
            for half in range(2):
                for i in range(len(pieces_of(k, cg))):
                    tile, copy = part_send(k, cg, half, i)

                    @pl.when(tile != t)
                    def _():
                        copy().wait_send()

        for dz in range(1, 4):
            sums_copy(k, dz).wait_send()
    for dz in range(1, 4):
        peer = (t + dz) % 4
        tile_copy(bands.at[peer], bands_in.at[3 - dz], bs_sem.at[dz - 1], br_sem.at[3 - dz], peer).wait_send()


def exchange(sorted_frames, members, ages):
    slot = sorted_frames.shape[2]
    vmem = pl.BlockSpec(memory_space=pltpu.VMEM)
    f32 = jnp.float32
    dma = pltpu.SemaphoreType.DMA
    return pl.pallas_call(
        exchange_kernel,
        out_shape=[
            jax.ShapeDtypeStruct((256, 1024), f32),
            jax.ShapeDtypeStruct((NA, 256), f32),
            jax.ShapeDtypeStruct((1, slot), f32),
        ],
        in_specs=[pl.BlockSpec(memory_space=pl.ANY), vmem, vmem],
        out_specs=[vmem] * 3,
        scratch_shapes=[
            pltpu.VMEM((1024, slot), jnp.bfloat16),
            pltpu.VMEM((4, 4, 2, 256, 128), f32),
            pltpu.VMEM((4, 2, 3, 256, 128), f32),
            pltpu.VMEM((4, 2, 256, 128), f32),
            pltpu.VMEM((2, 8, 128, 128), f32),
            pltpu.VMEM((4, 8, 384), f32),
            pltpu.VMEM((4, 3, 8, 384), f32),
            pltpu.VMEM((4, NA, 256), f32),
            pltpu.VMEM((3, NA, 256), f32),
            dma(()),
            dma((16, 2)),
            dma((32,)),
            dma((4, 4, 2, 3)),
            dma((4, 2, 3, 3)),
            dma((4, 2, 4)),
            dma((2, 8, 2)),
            dma((4, 3)),
            dma((4, 3)),
            dma((3,)),
            dma((3,)),
        ],
        compiler_params=pltpu.CompilerParams(collective_id=0, has_side_effects=True, vmem_limit_bytes=51 << 20),
    )(sorted_frames, members, ages)


def local(counts, dark_level, flat_field, valid_pixel, cycle_label, cycle_order, age_bin):
    table = (dark_level.shape[0] // BLK, BLK)
    sorted_frames, members = sort_frames(
        cycle_order[0],
        counts,
        dark_level.reshape(table),
        flat_field.reshape(table),
        valid_pixel.reshape(table),
        cycle_label.reshape(table),
    )
    two_time, aged, image = exchange(sorted_frames, members, age_bin[None, :])
    return (two_time[None], aged[None], image[None])


def solution(mesh):
    in_specs = (
        P("frame", "tile"),
        P("tile"),
        P("tile"),
        P("tile"),
        P("tile"),
        P("tile", None, None),
        P(),
    )
    out_specs = (P("frame", "tile", None), P("frame", None, "tile"), P("tile", "frame", None))
    return jax.shard_map(local, mesh=mesh, in_specs=in_specs, out_specs=out_specs, check_vma=False)
```
